32 devices in a mesh: grp: 2 (over y), row: 4 (over z), col: 2 (over x), half: 2 (over core).
Axes of the slice: x: 2, y: 2, z: 4, core: 2. Of those that a mesh axis runs over, the one named last changes fastest.
Arguments:
- vecs: bfloat16 [4, 1024, 32768], P(('grp', 'half'), 'row', 'col'), parts along dimension 0, may hold values from -6 to 6
- poles: float32 [4, 32768], P(('grp', 'half'), 'col'), parts along dimension 0, may hold values from -512 to 512, as said below
- weights: float32 [4, 32768], P(('grp', 'half'), 'col'), parts along dimension 0, may hold values from -5 to 5
- kept: int32 [4, 32768], P(('grp', 'half'), 'col'), parts along dimension 0, may hold values 0 or 1
- roots: float32 [1024], P(('grp', 'row')), parts along dimension 0, may hold values from -512 to 512, as said below
- order: int32 [1024], P('grp'), parts along dimension 0, may hold values from 0 to 511, each once
Outputs:
- merged: bfloat16 [16, 4, 2, 32, 512], P(('grp', 'row', 'half'), None, None, None, 'col'), parts along dimension 0
The draws below stay inside these ranges and needn't reach their ends.
There are 2 independent parts, one for each index of `grp`. The reference program is written for one: setup_inputs(seed, part) draws one part's arguments, and reference() takes and returns one part's arrays. A program takes and returns all parts, laid end to end along the dimension named above; each array names one. Nothing has to cross between parts.
Inputs may be any that keep to these rules, and one draw needn't show every extreme that they name: `poles`: every root differs from every pole by 0.2 or more. `roots`: every root differs from every pole by 0.2 or more. `order`: A permutation of 0 to 511.
All inputs are finite; a program needn't handle non-finite values. No bound on the sum of `kept` on one device may be relied on, other than what follows from the above.
Results may differ from the reference program's by a relative error of at most 0.0049.
Values may be sent and summed in bfloat16 or wider, within the bound.
A program may use at most 64 MiB of HBM per device.

```python
import jax
import jax.numpy as jnp
from jax import lax

NH = 32768
PANEL = 512
BINS = 1024
QROWS = 1024
BS = 32
N_ROW = 4


def draw_poles(key, part):
    first = jax.random.fold_in(key, 11)
    second = jax.random.fold_in(key, 12)
    levels = jax.random.randint(first, (2, NH), -(BINS // 2), BINS // 2)
    frac = jax.random.uniform(second, (2, NH), jnp.float32, 0.0, 0.3)
    return levels.astype(jnp.float32) + frac


def draw_roots(key, part):
    first = jax.random.fold_in(key, 21)
    second = jax.random.fold_in(key, 22)
    levels = jax.random.randint(first, (PANEL,), -(BINS // 2), BINS // 2 - 1)
    frac = jax.random.uniform(second, (PANEL,), jnp.float32, 0.5, 0.8)
    return levels.astype(jnp.float32) + frac


def place_ends(drawn, stream_key, least, largest):
    extent = drawn.shape
    place = [jax.random.randint(jax.random.fold_in(stream_key, axis), (), 0, extent[axis]) for axis in range(len(extent))]
    drawn = drawn.at[tuple(place)].set(least)
    longest = extent.index(max(extent))
    place[longest] = (place[longest] + 1) % extent[longest]
    return drawn.at[tuple(place)].set(largest)


def shard_levels(key, extent, split, smallest, largest):
    loudness = 1.0
    for dim, blocks in split:
        draws = jax.random.uniform(jax.random.fold_in(jax.random.fold_in(key, 6), dim), (blocks,), jnp.float32, smallest / len(split), largest / len(split))
        loudness = loudness * jnp.repeat(jnp.exp(draws), extent[dim] // blocks).reshape((-1,) + (1,) * (len(extent) - 1 - dim))
    return loudness


def bell_draw(stream_key, dims, width, limit, shards=(), dtype=jnp.bfloat16):
    level = shard_levels(stream_key, dims, shards, -0.22, 0.18) if shards else 1.0
    drawn = jax.random.normal(stream_key, dims, jnp.float32) * width * level
    return jnp.minimum(jnp.maximum(drawn, -limit), limit).astype(dtype)


def setup_inputs(seed: int = 0, part: int = 0) -> dict:
    keys = jax.random.split(jax.random.key(seed), 7)
    part_splits = jax.random.split(jax.random.fold_in(keys[6], part), 7)
    return {
        "vecs": bell_draw(part_splits[0], (2, QROWS, NH), 1.0, 6.0, ((0, 2), (1, 4), (2, 2))),
        "poles": draw_poles(jax.random.fold_in(jax.random.fold_in(keys[6], part), 71), part),
        "weights": bell_draw(part_splits[2], (2, NH), 1.0, 5.0, ((0, 2), (1, 2)), jnp.float32),
        "kept": place_ends((jax.random.randint(part_splits[3], (2, NH), 0, 4) < 3).astype(jnp.int32), jax.random.fold_in(part_splits[3], 1), 0, 1),
        "roots": draw_roots(jax.random.fold_in(jax.random.fold_in(keys[6], part), 71), part),
        "order": jax.random.permutation(part_splits[5], PANEL).astype(jnp.int32),
    }


def reference(vecs, poles, weights, kept, roots, order):
    theta = roots[order.astype(jnp.int32)]
    scaled = weights * kept.astype(jnp.float32)
    cauchy = scaled[:, :, None] / (poles[:, :, None] - theta[None, None, :])
    norms = lax.optimization_barrier(jnp.sum(cauchy * cauchy, axis=(0, 1)))
    zpanel = (cauchy * lax.rsqrt(norms + 1e-06)).astype(jnp.bfloat16)
    upper = jnp.dot(vecs[0], zpanel[0], preferred_element_type=jnp.float32).astype(jnp.bfloat16)
    lower = jnp.dot(vecs[1], zpanel[1], preferred_element_type=jnp.float32).astype(jnp.bfloat16)
    product = jnp.stack([upper, lower], axis=0)
    blocks = product.reshape(2, N_ROW, 2 * N_ROW, BS, PANEL)
    return jnp.transpose(blocks, (2, 1, 0, 3, 4))
```

```python
import functools

import jax
import jax.numpy as jnp
from jax import lax
from jax.experimental import pallas as pl
from jax.experimental.pallas import tpu as pltpu
from jax.sharding import PartitionSpec as P

MESH = pl.DeviceIdType.MESH
LANES = 128


def kernel(dims, vecs, poles, weights, kept, roots, order, out,
           vbuf, rootbuf, theta, scaled, zbuf, acc, nacc, psend, precv, nsend, nrecv, asend, arecv,
           vsem, rsend, rrecv, pssem, prsem, nssem, nrsem, assem, arsem):
    n_row, n_col, n_half, cols, panel, block, sub = dims
    grp, row, col, half = (lax.axis_index(a) for a in ("grp", "row", "col", "half"))
    share = panel // n_col
    width = panel // n_row
    nrows = vbuf.shape[0]
    groups = n_row * n_half
    depth = nrows // groups
    n_blocks = cols // block

    def load(i):
        at = pl.ds(pl.multiple_of(i * block, block), block)
        return pltpu.make_async_copy(vecs.at[0, :, at], vbuf.at[:, at], vsem.at[i])

    for i in range(n_blocks):
        load(i).start()

    me = row * n_half + half
    barrier = pltpu.get_barrier_semaphore()
    for o in range(1, groups):
        g = lax.rem(me + o, groups)
        pl.semaphore_signal(barrier, inc=1, device_id=(grp, g // n_half, col, lax.rem(g, n_half)), device_id_type=MESH)
    for t in range(1, n_col):
        for h in range(n_half):
            pl.semaphore_signal(barrier, inc=1, device_id=(grp, row, lax.rem(col + t, n_col), h), device_id_type=MESH)

    scaled[...] = weights[...] * kept[...].astype(jnp.float32)
    order_col = jnp.transpose(jnp.broadcast_to(order[...], (8, panel)))[:, :1]

    pl.semaphore_wait(barrier, groups - 1 + (n_col - 1) * n_half)

    def root_copy(o):
        return pltpu.make_async_remote_copy(
            src_ref=roots, dst_ref=rootbuf.at[o], send_sem=rsend.at[o], recv_sem=rrecv.at[o],
            device_id=(grp, lax.rem(row + o, n_row), col, half), device_id_type=MESH)

    for o in range(1, n_row):
        root_copy(o).start()
    lane = lax.broadcasted_iota(jnp.int32, (panel, width), 1)
    picked = jnp.zeros((panel, width), jnp.float32)
    for o in range(n_row):
        if o:
            root_copy(o).wait()
        source = lax.rem(row + n_row - o, n_row)
        block_roots = rootbuf[o] if o else roots[...]
        picked = jnp.where(order_col - source * width == lane, block_roots, picked)
    theta[...] = jnp.broadcast_to(jnp.sum(picked, axis=1, keepdims=True), (panel, LANES))

    def chunk(t):
        base = pl.multiple_of(lax.rem(col + t, n_col) * share, share)
        acc[...] = jnp.zeros_like(acc)
        nacc[...] = jnp.zeros_like(nacc)

        def step(i, carry):
            if t == 1 or n_col == 1:
                load(i).wait()
            start = pl.multiple_of(i * block, block)
            total = acc[...]
            for s in range(block // sub):
                for k in range(0, share, 16):
                    th = theta[pl.ds(base + k, 16), :]
                    squares = nacc[k:k + 16, :]
                    for c in range(s * sub, (s + 1) * sub, LANES):
                        at = pl.ds(start + c, LANES)
                        cauchy = scaled[:, at] / (poles[:, at] - th)
                        squares += cauchy * cauchy
                        zbuf[k:k + 16, c:c + LANES] = cauchy.astype(jnp.bfloat16)
                    nacc[k:k + 16, :] = squares
                total += lax.dot_general(
                    vbuf[:, pl.ds(start + s * sub, sub)], zbuf[:, s * sub:(s + 1) * sub],
                    (((1,), (1,)), ((), ())), preferred_element_type=jnp.float32)
            acc[...] = total
            return carry

        lax.fori_loop(0, n_blocks, step, 0)
        nsend[t] = jnp.sum(jnp.transpose(nacc[...]), axis=0, keepdims=True)

    def norm_copy(t, o):
        return pltpu.make_async_remote_copy(
            src_ref=nsend.at[t], dst_ref=nrecv.at[t, o], send_sem=nssem.at[t, o], recv_sem=nrsem.at[t, o],
            device_id=(grp, row, lax.rem(col + t, n_col), lax.rem(half + o, n_half)), device_id_type=MESH)

    def part_copy(t):
        return pltpu.make_async_remote_copy(
            src_ref=psend.at[t - 1], dst_ref=precv.at[t - 1], send_sem=pssem.at[t - 1], recv_sem=prsem.at[t - 1],
            device_id=(grp, row, lax.rem(col + t, n_col), half), device_id_type=MESH)

    def piece_copy(o):
        g = lax.rem(me + o, groups)
        return pltpu.make_async_remote_copy(
            src_ref=asend.at[g], dst_ref=arecv.at[o], send_sem=assem.at[o], recv_sem=arsem.at[o],
            device_id=(grp, g // n_half, col, lax.rem(g, n_half)), device_id_type=MESH)

    norm_copies = [(t, o) for t in range(n_col) for o in range(n_half) if t or o]
    for t in range(1, n_col):
        chunk(t)
        psend[t - 1] = acc[...].astype(jnp.bfloat16)
        part_copy(t).start()
        for o in range(n_half):
            norm_copy(t, o).start()
    chunk(0)
    for o in range(1, n_half):
        norm_copy(0, o).start()
    total = acc[...]
    for t in range(1, n_col):
        part_copy(t).wait()
        total += precv[t - 1].astype(jnp.float32)
    asend[...] = total.reshape(groups, depth, share).astype(jnp.bfloat16)
    for o in range(1, groups):
        piece_copy(o).start()
    norms = nsend[0]
    for t, o in norm_copies:
        norm_copy(t, o).wait()
        norms += nrecv[t, o]
    scale = lax.rsqrt(norms + 1e-06)
    for o in range(groups):
        if o:
            piece_copy(o).wait()
        g = lax.rem(me + groups - o, groups)
        piece = arecv[o] if o else asend[me]
        out[0, g // n_half, lax.rem(g, n_half)] = (piece.astype(jnp.float32) * scale).astype(jnp.bfloat16)


def body(vecs, poles, weights, kept, roots, order):
    n_row, n_col, n_half = (lax.axis_size(a) for a in ("row", "col", "half"))
    nrows, cols = vecs.shape[1:]
    panel = order.shape[0]
    share, groups = panel // n_col, n_row * n_half
    depth = nrows // groups
    block = min(2048, cols)
    sub = min(512, block)
    vmem = pl.BlockSpec(memory_space=pltpu.VMEM)
    dma = pltpu.SemaphoreType.DMA
    others = max(n_col - 1, 1)
    return pl.pallas_call(
        functools.partial(kernel, (n_row, n_col, n_half, cols, panel, block, sub)),
        out_shape=jax.ShapeDtypeStruct((1, n_row, n_half, depth, share), jnp.bfloat16),
        in_specs=[pl.BlockSpec(memory_space=pl.ANY)] + [vmem] * 5,
        out_specs=vmem,
        scratch_shapes=[
            pltpu.VMEM((nrows, cols), jnp.bfloat16),
            pltpu.VMEM((n_row, 1, panel // n_row), jnp.float32),
            pltpu.VMEM((panel, LANES), jnp.float32),
            pltpu.VMEM((1, cols), jnp.float32),
            pltpu.VMEM((share, block), jnp.bfloat16),
            pltpu.VMEM((nrows, share), jnp.float32),
            pltpu.VMEM((share, LANES), jnp.float32),
            pltpu.VMEM((others, nrows, share), jnp.bfloat16),
            pltpu.VMEM((others, nrows, share), jnp.bfloat16),
            pltpu.VMEM((n_col, 1, share), jnp.float32),
            pltpu.VMEM((n_col, n_half, 1, share), jnp.float32),
            pltpu.VMEM((groups, depth, share), jnp.bfloat16),
            pltpu.VMEM((groups, depth, share), jnp.bfloat16),
            dma((cols // block,)),
            dma((n_row,)),
            dma((n_row,)),
            dma((others,)),
            dma((others,)),
            dma((n_col, n_half)),
            dma((n_col, n_half)),
            dma((groups,)),
            dma((groups,)),
        ],
        compiler_params=pltpu.CompilerParams(collective_id=0, has_side_effects=True),
        name="merge",
    )(vecs, poles, weights, kept, roots[None, :], order[None, :])


def solution(mesh):
    return jax.shard_map(
        body,
        mesh=mesh,
        in_specs=(
            P(("grp", "half"), "row", "col"),
            P(("grp", "half"), "col"),
            P(("grp", "half"), "col"),
            P(("grp", "half"), "col"),
            P(("grp", "row")),
            P("grp"),
        ),
        out_specs=P(("grp", "row", "half"), None, None, None, "col"),
        check_vma=False,
    )
```

```python
import functools

import jax
import jax.numpy as jnp
from jax import lax
from jax.experimental import pallas as pl
from jax.experimental.pallas import tpu as pltpu
from jax.sharding import PartitionSpec as P

MESH = pl.DeviceIdType.MESH
LANES = 128


def kernel(dims, vecs, poles, weights, kept, roots, order, out,
           vbuf, rootbuf, theta, scaled, zbuf, acc, nacc, psend, precv, nsend, nrecv, asend, arecv,
           vsem, rsend, rrecv, pssem, prsem, nssem, nrsem, assem, arsem):
    n_row, n_col, n_half, cols, panel, block, sub = dims
    grp, row, col, half = (lax.axis_index(a) for a in ("grp", "row", "col", "half"))
    share = panel // n_col
    width = panel // n_row
    nrows = vbuf.shape[1]
    groups = n_row * n_half
    depth = nrows // groups
    n_blocks = cols // block

    tiles = block // LANES

    def tile_load(i, j):
        at = pl.ds(pl.multiple_of(i * block + j * LANES, LANES), LANES)
        return pltpu.make_async_copy(vecs.at[0, :, at], vbuf.at[i * tiles + j], vsem.at[i])

    def loaded(i):
        here = vbuf.at[pl.ds(i * tiles, tiles)]
        pltpu.make_async_copy(here, here, vsem.at[i]).wait()

    me = row * n_half + half
    barrier = pltpu.get_barrier_semaphore()
    for o in range(1, groups):
        g = lax.rem(me + o, groups)
        pl.semaphore_signal(barrier, inc=1, device_id=(grp, g // n_half, col, lax.rem(g, n_half)), device_id_type=MESH)
    for t in range(1, n_col):
        for h in range(n_half):
            pl.semaphore_signal(barrier, inc=1, device_id=(grp, row, lax.rem(col + t, n_col), h), device_id_type=MESH)

    for i in range(n_blocks):
        for j in range(tiles):
            tile_load(i, j).start()
    scaled[...] = weights[...] * kept[...].astype(jnp.float32)
    order_col = jnp.transpose(jnp.broadcast_to(order[...], (8, panel)))[:, :1]

    pl.semaphore_wait(barrier, groups - 1 + (n_col - 1) * n_half)

    def root_copy(o):
        return pltpu.make_async_remote_copy(
            src_ref=roots, dst_ref=rootbuf.at[o], send_sem=rsend.at[o], recv_sem=rrecv.at[o],
            device_id=(grp, lax.rem(row + o, n_row), col, half), device_id_type=MESH)

    for o in range(1, n_row):
        root_copy(o).start()
    lane = lax.broadcasted_iota(jnp.int32, (panel, width), 1)
    picked = jnp.zeros((panel, width), jnp.float32)
    for o in range(n_row):
        if o:
            root_copy(o).wait()
        source = lax.rem(row + n_row - o, n_row)
        block_roots = rootbuf[o] if o else roots[...]
        picked = jnp.where(order_col - source * width == lane, block_roots, picked)
    theta[...] = jnp.broadcast_to(jnp.sum(picked, axis=1, keepdims=True), (panel, LANES))

    def chunk(t):
        base = pl.multiple_of(lax.rem(col + t, n_col) * share, share)
        acc[...] = jnp.zeros_like(acc)
        nacc[...] = jnp.zeros_like(nacc)

        def step(i, carry):
            if t == 1 or n_col == 1:
                loaded(i)
            start = pl.multiple_of(i * block, block)
            total = acc[...]
            for s in range(block // sub):
                for k in range(0, share, 16):
                    th = theta[pl.ds(base + k, 16), :]
                    squares = nacc[k:k + 16, :]
                    for c in range(s * sub, (s + 1) * sub, LANES):
                        at = pl.ds(start + c, LANES)
                        cauchy = scaled[:, at] / (poles[:, at] - th)
                        squares += cauchy * cauchy
                        zbuf[c // LANES, k:k + 16, :] = cauchy.astype(jnp.bfloat16)
                    nacc[k:k + 16, :] = squares
                tile = range(s * sub // LANES, (s + 1) * sub // LANES)
                total += lax.dot_general(
                    jnp.concatenate([vbuf[i * tiles + j] for j in tile], axis=1),
                    jnp.concatenate([zbuf[j] for j in tile], axis=1),
                    (((1,), (1,)), ((), ())), preferred_element_type=jnp.float32)
            acc[...] = total
            return carry

        lax.fori_loop(0, n_blocks, step, 0)
        nsend[t] = jnp.sum(jnp.transpose(nacc[...]), axis=0, keepdims=True)

    def norm_copy(t, o):
        return pltpu.make_async_remote_copy(
            src_ref=nsend.at[t], dst_ref=nrecv.at[t, o], send_sem=nssem.at[t, o], recv_sem=nrsem.at[t, o],
            device_id=(grp, row, lax.rem(col + t, n_col), lax.rem(half + o, n_half)), device_id_type=MESH)

    def part_copy(t):
        return pltpu.make_async_remote_copy(
            src_ref=psend.at[t - 1], dst_ref=precv.at[t - 1], send_sem=pssem.at[t - 1], recv_sem=prsem.at[t - 1],
            device_id=(grp, row, lax.rem(col + t, n_col), half), device_id_type=MESH)

    def piece_copy(o):
        g = lax.rem(me + o, groups)
        return pltpu.make_async_remote_copy(
            src_ref=asend.at[g], dst_ref=arecv.at[o], send_sem=assem.at[o], recv_sem=arsem.at[o],
            device_id=(grp, g // n_half, col, lax.rem(g, n_half)), device_id_type=MESH)

    norm_copies = [(t, o) for t in range(n_col) for o in range(n_half) if t or o]
    for t in range(1, n_col):
        chunk(t)
        psend[t - 1] = acc[...].astype(jnp.bfloat16)
        part_copy(t).start()
        for o in range(n_half):
            norm_copy(t, o).start()
    chunk(0)
    for o in range(1, n_half):
        norm_copy(0, o).start()
    total = acc[...]
    for t in range(1, n_col):
        part_copy(t).wait()
        total += precv[t - 1].astype(jnp.float32)
    asend[...] = total.reshape(groups, depth, share).astype(jnp.bfloat16)
    for o in range(1, groups):
        piece_copy(o).start()
    norms = nsend[0]
    for t, o in norm_copies:
        norm_copy(t, o).wait()
        norms += nrecv[t, o]
    scale = lax.rsqrt(norms + 1e-06)
    for o in range(groups):
        if o:
            piece_copy(o).wait()
        g = lax.rem(me + groups - o, groups)
        piece = arecv[o] if o else asend[me]
        out[0, g // n_half, lax.rem(g, n_half)] = (piece.astype(jnp.float32) * scale).astype(jnp.bfloat16)


def body(vecs, poles, weights, kept, roots, order):
    n_row, n_col, n_half = (lax.axis_size(a) for a in ("row", "col", "half"))
    nrows, cols = vecs.shape[1:]
    panel = order.shape[0]
    share, groups = panel // n_col, n_row * n_half
    depth = nrows // groups
    block = min(2048, cols)
    sub = min(512, block)
    vmem = pl.BlockSpec(memory_space=pltpu.VMEM)
    dma = pltpu.SemaphoreType.DMA
    others = max(n_col - 1, 1)
    return pl.pallas_call(
        functools.partial(kernel, (n_row, n_col, n_half, cols, panel, block, sub)),
        out_shape=jax.ShapeDtypeStruct((1, n_row, n_half, depth, share), jnp.bfloat16),
        in_specs=[pl.BlockSpec(memory_space=pl.ANY)] + [vmem] * 5,
        out_specs=vmem,
        scratch_shapes=[
            pltpu.VMEM((cols // LANES, nrows, LANES), jnp.bfloat16),
            pltpu.VMEM((n_row, 1, panel // n_row), jnp.float32),
            pltpu.VMEM((panel, LANES), jnp.float32),
            pltpu.VMEM((1, cols), jnp.float32),
            pltpu.VMEM((block // LANES, share, LANES), jnp.bfloat16),
            pltpu.VMEM((nrows, share), jnp.float32),
            pltpu.VMEM((share, LANES), jnp.float32),
            pltpu.VMEM((others, nrows, share), jnp.bfloat16),
            pltpu.VMEM((others, nrows, share), jnp.bfloat16),
            pltpu.VMEM((n_col, 1, share), jnp.float32),
            pltpu.VMEM((n_col, n_half, 1, share), jnp.float32),
            pltpu.VMEM((groups, depth, share), jnp.bfloat16),
            pltpu.VMEM((groups, depth, share), jnp.bfloat16),
            dma((cols // block,)),
            dma((n_row,)),
            dma((n_row,)),
            dma((others,)),
            dma((others,)),
            dma((n_col, n_half)),
            dma((n_col, n_half)),
            dma((groups,)),
            dma((groups,)),
        ],
        compiler_params=pltpu.CompilerParams(collective_id=0, has_side_effects=True),
        name="merge",
    )(vecs, poles, weights, kept, roots[None, :], order[None, :])


def solution(mesh):
    return jax.shard_map(
        body,
        mesh=mesh,
        in_specs=(
            P(("grp", "half"), "row", "col"),
            P(("grp", "half"), "col"),
            P(("grp", "half"), "col"),
            P(("grp", "half"), "col"),
            P(("grp", "row")),
            P("grp"),
        ),
        out_specs=P(("grp", "row", "half"), None, None, None, "col"),
        check_vma=False,
    )
```

```python
import functools

import jax
import jax.numpy as jnp
from jax import lax
from jax.experimental import pallas as pl
from jax.experimental.pallas import tpu as pltpu
from jax.sharding import PartitionSpec as P

MESH = pl.DeviceIdType.MESH
LANES = 128


def kernel(dims, vecs, poles, weights, kept, roots, order, out,
           vbuf, rootbuf, theta, scaled, picks, raw, mask, centers, own, zeven, zodd, acc, nacc, psend, precv, nsend, nrecv, asend, arecv,
           ssem, vsem, rsend, rrecv, pssem, prsem, nssem, nrsem, assem, arsem):
    n_row, n_col, n_half, cols, panel, block, rows = dims
    grp, row, col, half = (lax.axis_index(a) for a in ("grp", "row", "col", "half"))
    share = panel // n_col
    width = panel // n_row
    nrows = vbuf.shape[1]
    groups = n_row * n_half
    depth = nrows // groups
    n_blocks = cols // block

    tiles = block // LANES

    def tile_load(i, j):
        at = pl.ds(pl.multiple_of(i * block + j * LANES, LANES), LANES)
        return pltpu.make_async_copy(vecs.at[0, :, at], vbuf.at[i * tiles + j], vsem.at[i])

    def loaded(i):
        here = vbuf.at[pl.ds(i * tiles, tiles)]
        pltpu.make_async_copy(here, here, vsem.at[i]).wait()

    me = row * n_half + half
    barrier = pltpu.get_barrier_semaphore()
    for o in range(1, groups):
        g = lax.rem(me + o, groups)
        pl.semaphore_signal(barrier, inc=1, device_id=(grp, g // n_half, col, lax.rem(g, n_half)), device_id_type=MESH)
    for t in range(1, n_col):
        for h in range(n_half):
            pl.semaphore_signal(barrier, inc=1, device_id=(grp, row, lax.rem(col + t, n_col), h), device_id_type=MESH)

    small = [(order, picks), (weights, raw), (kept, mask), (poles, centers), (roots, own)]
    fetches = [pltpu.make_async_copy(src, dst, ssem.at[n]) for n, (src, dst) in enumerate(small)]
    for fetch in fetches:
        fetch.start()

    for i in range(n_blocks):
        for j in range(tiles):
            tile_load(i, j).start()
    acc[...] = jnp.zeros_like(acc)
    zodd[...] = jnp.zeros_like(zodd)
    pl.semaphore_wait(barrier, groups - 1 + (n_col - 1) * n_half)

    def root_copy(o):
        return pltpu.make_async_remote_copy(
            src_ref=roots, dst_ref=rootbuf.at[o], send_sem=rsend.at[o], recv_sem=rrecv.at[o],
            device_id=(grp, lax.rem(row + o, n_row), col, half), device_id_type=MESH)

    for o in range(1, n_row):
        root_copy(o).start()
    for fetch in fetches:
        fetch.wait()
    scaled[...] = raw[...] * mask[...].astype(jnp.float32)
    wanted = jnp.transpose(jnp.broadcast_to(picks[...], (LANES, panel)))[:, :width]
    lane = lax.broadcasted_iota(jnp.int32, (panel, width), 1)
    picked = jnp.zeros((panel, width), jnp.float32)
    for o in range(n_row):
        if o:
            root_copy(o).wait()
        source = lax.rem(row + n_row - o, n_row)
        picked = jnp.where(wanted - source * width == lane, rootbuf[o] if o else own[...], picked)
    theta[...] = jnp.broadcast_to(jnp.sum(picked, axis=1, keepdims=True), (panel, LANES))

    strips = share // rows
    span = tiles // strips

    def dot(z, i, k):
        acc[...] += lax.dot_general(
            jnp.concatenate([vbuf[i * tiles + k * span + j] for j in range(span)], axis=1),
            jnp.concatenate([z[k * span + j] for j in range(span)], axis=1),
            (((1,), (1,)), ((), ())), preferred_element_type=jnp.float32)

    def chunk(t):
        base = lax.rem(col + t, n_col) * share
        nacc[...] = jnp.zeros_like(nacc)

        def fill(z, i, k):
            first = pl.multiple_of(k * rows, rows)
            th = [theta[pl.ds(pl.multiple_of(base + k * rows + r, 16), 16), :] for r in range(0, rows, 16)]
            squares = [nacc[pl.ds(first + r, 16), :] for r in range(0, rows, 16)]
            for j in range(tiles):
                at = pl.ds(pl.multiple_of(i * block + j * LANES, LANES), LANES)
                weight, center = scaled[:, at], centers[:, at]
                for n in range(rows // 16):
                    cauchy = weight / (center - th[n])
                    squares[n] += cauchy * cauchy
                    z[j, pl.ds(first + n * 16, 16), :] = cauchy.astype(jnp.bfloat16)
            for n in range(rows // 16):
                nacc[pl.ds(first + n * 16, 16), :] = squares[n]

        def pair(p, carry):
            def even(k, carry):
                dot(zodd, jnp.maximum(2 * p - 1, 0), k)
                fill(zeven, 2 * p, k)
                return carry

            def odd(k, carry):
                dot(zeven, 2 * p, k)
                fill(zodd, 2 * p + 1, k)
                return carry

            if t == 1 or n_col == 1:
                loaded(2 * p)
                loaded(2 * p + 1)
            lax.fori_loop(0, strips, even, 0)

            @pl.when(p == 0)
            def _():
                acc[...] = jnp.zeros_like(acc)

            lax.fori_loop(0, strips, odd, 0)
            return carry

        lax.fori_loop(0, n_blocks // 2, pair, 0)

        def rest(k, carry):
            dot(zodd, n_blocks - 1, k)
            return carry

        lax.fori_loop(0, strips, rest, 0)
        nsend[t] = jnp.sum(jnp.transpose(nacc[...]), axis=0, keepdims=True)

    def norm_copy(t, o):
        return pltpu.make_async_remote_copy(
            src_ref=nsend.at[t], dst_ref=nrecv.at[t, o], send_sem=nssem.at[t, o], recv_sem=nrsem.at[t, o],
            device_id=(grp, row, lax.rem(col + t, n_col), lax.rem(half + o, n_half)), device_id_type=MESH)

    def part_copy(t):
        return pltpu.make_async_remote_copy(
            src_ref=psend.at[t - 1], dst_ref=precv.at[t - 1], send_sem=pssem.at[t - 1], recv_sem=prsem.at[t - 1],
            device_id=(grp, row, lax.rem(col + t, n_col), half), device_id_type=MESH)

    def piece_copy(o):
        g = lax.rem(me + o, groups)
        return pltpu.make_async_remote_copy(
            src_ref=asend.at[g], dst_ref=arecv.at[o], send_sem=assem.at[o], recv_sem=arsem.at[o],
            device_id=(grp, g // n_half, col, lax.rem(g, n_half)), device_id_type=MESH)

    norm_copies = [(t, o) for t in range(n_col) for o in range(n_half) if t or o]
    for t in range(1, n_col):
        chunk(t)
        psend[t - 1] = acc[...].astype(jnp.bfloat16)
        part_copy(t).start()
        for o in range(n_half):
            norm_copy(t, o).start()
    chunk(0)
    for o in range(1, n_half):
        norm_copy(0, o).start()
    total = acc[...]
    for t in range(1, n_col):
        part_copy(t).wait()
        total += precv[t - 1].astype(jnp.float32)
    asend[...] = total.reshape(groups, depth, share).astype(jnp.bfloat16)
    for o in range(1, groups):
        piece_copy(o).start()
    norms = nsend[0]
    for t, o in norm_copies:
        norm_copy(t, o).wait()
        norms += nrecv[t, o]
    scale = lax.rsqrt(norms + 1e-06)
    for o in range(groups):
        if o:
            piece_copy(o).wait()
        g = lax.rem(me + groups - o, groups)
        piece = arecv[o] if o else asend[me]
        out[0, g // n_half, lax.rem(g, n_half)] = (piece.astype(jnp.float32) * scale).astype(jnp.bfloat16)


def body(vecs, poles, weights, kept, roots, order):
    n_row, n_col, n_half = (lax.axis_size(a) for a in ("row", "col", "half"))
    nrows, cols = vecs.shape[1:]
    panel = order.shape[0]
    share, groups = panel // n_col, n_row * n_half
    depth = nrows // groups
    block = min(4096, cols // 2)
    rows = min(128, share)
    vmem = pl.BlockSpec(memory_space=pltpu.VMEM)
    dma = pltpu.SemaphoreType.DMA
    others = max(n_col - 1, 1)
    return pl.pallas_call(
        functools.partial(kernel, (n_row, n_col, n_half, cols, panel, block, rows)),
        out_shape=jax.ShapeDtypeStruct((1, n_row, n_half, depth, share), jnp.bfloat16),
        in_specs=[pl.BlockSpec(memory_space=pl.ANY)] * 6,
        out_specs=vmem,
        scratch_shapes=[
            pltpu.VMEM((cols // LANES, nrows, LANES), jnp.bfloat16),
            pltpu.VMEM((n_row, 1, panel // n_row), jnp.float32),
            pltpu.VMEM((panel, LANES), jnp.float32),
            pltpu.VMEM((1, cols), jnp.float32),
            pltpu.VMEM((1, panel), jnp.int32),
            pltpu.VMEM((1, cols), jnp.float32),
            pltpu.VMEM((1, cols), jnp.int32),
            pltpu.VMEM((1, cols), jnp.float32),
            pltpu.VMEM((1, panel // n_row), jnp.float32),
            pltpu.VMEM((block // LANES, share, LANES), jnp.bfloat16),
            pltpu.VMEM((block // LANES, share, LANES), jnp.bfloat16),
            pltpu.VMEM((nrows, share), jnp.float32),
            pltpu.VMEM((share, LANES), jnp.float32),
            pltpu.VMEM((others, nrows, share), jnp.bfloat16),
            pltpu.VMEM((others, nrows, share), jnp.bfloat16),
            pltpu.VMEM((n_col, 1, share), jnp.float32),
            pltpu.VMEM((n_col, n_half, 1, share), jnp.float32),
            pltpu.VMEM((groups, depth, share), jnp.bfloat16),
            pltpu.VMEM((groups, depth, share), jnp.bfloat16),
            dma((5,)),
            dma((cols // block,)),
            dma((n_row,)),
            dma((n_row,)),
            dma((others,)),
            dma((others,)),
            dma((n_col, n_half)),
            dma((n_col, n_half)),
            dma((groups,)),
            dma((groups,)),
        ],
        compiler_params=pltpu.CompilerParams(collective_id=0, has_side_effects=True),
        name="merge",
    )(vecs, poles, weights, kept, roots[None, :], order[None, :])


def solution(mesh):
    return jax.shard_map(
        body,
        mesh=mesh,
        in_specs=(
            P(("grp", "half"), "row", "col"),
            P(("grp", "half"), "col"),
            P(("grp", "half"), "col"),
            P(("grp", "half"), "col"),
            P(("grp", "row")),
            P("grp"),
        ),
        out_specs=P(("grp", "row", "half"), None, None, None, "col"),
        check_vma=False,
    )
```

```python
import functools

import jax
import jax.numpy as jnp
from jax import lax
from jax.experimental import pallas as pl
from jax.experimental.pallas import tpu as pltpu
from jax.sharding import PartitionSpec as P

MESH = pl.DeviceIdType.MESH
LANES = 128


def kernel(dims, vecs, poles, weights, kept, roots, order, out,
           vbuf, rootbuf, theta, scaled, picks, raw, mask, centers, own, zeven, zodd, acc, nacc, psend, precv, nsend, nrecv, asend, arecv,
           ssem, vsem, rsend, rrecv, pssem, prsem, nssem, nrsem, assem, arsem):
    n_row, n_col, n_half, cols, panel, block, rows = dims
    grp, row, col, half = (lax.axis_index(a) for a in ("grp", "row", "col", "half"))
    share = panel // n_col
    width = panel // n_row
    nrows = vbuf.shape[1]
    groups = n_row * n_half
    depth = nrows // groups
    n_blocks = cols // block

    tiles = block // LANES

    def tile_load(i, j):
        at = pl.ds(pl.multiple_of(i * block + j * LANES, LANES), LANES)
        return pltpu.make_async_copy(vecs.at[0, :, at], vbuf.at[i * tiles + j], vsem.at[i])

    def loaded(i):
        here = vbuf.at[pl.ds(i * tiles, tiles)]
        pltpu.make_async_copy(here, here, vsem.at[i]).wait()

    me = row * n_half + half
    barrier = pltpu.get_barrier_semaphore()
    for o in range(1, groups):
        g = lax.rem(me + o, groups)
        pl.semaphore_signal(barrier, inc=1, device_id=(grp, g // n_half, col, lax.rem(g, n_half)), device_id_type=MESH)
    for t in range(1, n_col):
        for h in range(n_half):
            pl.semaphore_signal(barrier, inc=1, device_id=(grp, row, lax.rem(col + t, n_col), h), device_id_type=MESH)

    small = [(order, picks), (weights, raw), (kept, mask), (poles, centers), (roots, own)]
    fetches = [pltpu.make_async_copy(src, dst, ssem.at[n]) for n, (src, dst) in enumerate(small)]
    for fetch in fetches:
        fetch.start()

    for i in range(n_blocks):
        for j in range(tiles):
            tile_load(i, j).start()
    acc[...] = jnp.zeros_like(acc)
    zodd[...] = jnp.zeros_like(zodd)
    pl.semaphore_wait(barrier, groups - 1 + (n_col - 1) * n_half)

    def root_copy(o):
        return pltpu.make_async_remote_copy(
            src_ref=roots, dst_ref=rootbuf.at[o], send_sem=rsend.at[o], recv_sem=rrecv.at[o],
            device_id=(grp, lax.rem(row + o, n_row), col, half), device_id_type=MESH)

    for o in range(1, n_row):
        root_copy(o).start()
    for fetch in fetches:
        fetch.wait()
    scaled[...] = raw[...] * mask[...].astype(jnp.float32)
    wanted = jnp.transpose(jnp.broadcast_to(picks[...], (LANES, panel)))[:, :width]
    lane = lax.broadcasted_iota(jnp.int32, (panel, width), 1)
    picked = jnp.zeros((panel, width), jnp.float32)
    for o in range(n_row):
        if o:
            root_copy(o).wait()
        source = lax.rem(row + n_row - o, n_row)
        picked = jnp.where(wanted - source * width == lane, rootbuf[o] if o else own[...], picked)
    theta[...] = jnp.broadcast_to(jnp.sum(picked, axis=1, keepdims=True), (panel, LANES))

    strips = share // rows
    span = tiles // strips

    def dot(z, i, k):
        acc[...] += lax.dot_general(
            jnp.concatenate([vbuf[i * tiles + k * span + j] for j in range(span)], axis=1),
            jnp.concatenate([z[k * span + j] for j in range(span)], axis=1),
            (((1,), (1,)), ((), ())), preferred_element_type=jnp.float32)

    def chunk(t):
        base = lax.rem(col + t, n_col) * share
        nacc[...] = jnp.zeros_like(nacc)

        def fill(z, i, k):
            first = pl.multiple_of(k * rows, rows)
            th = [theta[pl.ds(pl.multiple_of(base + k * rows + r, 16), 16), :] for r in range(0, rows, 16)]
            squares = [nacc[pl.ds(first + r, 16), :] for r in range(0, rows, 16)]
            for j in range(tiles):
                at = pl.ds(pl.multiple_of(i * block + j * LANES, LANES), LANES)
                weight, center = scaled[:, at], centers[:, at]
                for n in range(rows // 16):
                    cauchy = weight / (center - th[n])
                    squares[n] += cauchy * cauchy
                    z[j, pl.ds(first + n * 16, 16), :] = cauchy.astype(jnp.bfloat16)
            for n in range(rows // 16):
                nacc[pl.ds(first + n * 16, 16), :] = squares[n]

        def pair(p, carry):
            def even(k, carry):
                dot(zodd, jnp.maximum(2 * p - 1, 0), k)
                fill(zeven, 2 * p, k)
                return carry

            def odd(k, carry):
                dot(zeven, 2 * p, k)
                fill(zodd, 2 * p + 1, k)
                return carry

            if t == 1 or n_col == 1:
                loaded(2 * p)
                loaded(2 * p + 1)
            lax.fori_loop(0, strips, even, 0)

            @pl.when(p == 0)
            def _():
                acc[...] = jnp.zeros_like(acc)

            lax.fori_loop(0, strips, odd, 0)
            return carry

        lax.fori_loop(0, n_blocks // 2, pair, 0)

        def rest(k, carry):
            dot(zodd, n_blocks - 1, k)
            return carry

        lax.fori_loop(0, strips, rest, 0)
        nsend[t] = jnp.sum(jnp.transpose(nacc[...]), axis=0, keepdims=True)

    def norm_copy(t, o):
        return pltpu.make_async_remote_copy(
            src_ref=nsend.at[t], dst_ref=nrecv.at[t, o], send_sem=nssem.at[t, o], recv_sem=nrsem.at[t, o],
            device_id=(grp, row, lax.rem(col + t, n_col), lax.rem(half + o, n_half)), device_id_type=MESH)

    def part_copy(t):
        return pltpu.make_async_remote_copy(
            src_ref=psend.at[t - 1], dst_ref=precv.at[t - 1], send_sem=pssem.at[t - 1], recv_sem=prsem.at[t - 1],
            device_id=(grp, row, lax.rem(col + t, n_col), half), device_id_type=MESH)

    def piece_copy(o):
        g = lax.rem(me + o, groups)
        return pltpu.make_async_remote_copy(
            src_ref=asend.at[g], dst_ref=arecv.at[o], send_sem=assem.at[o], recv_sem=arsem.at[o],
            device_id=(grp, g // n_half, col, lax.rem(g, n_half)), device_id_type=MESH)

    norm_copies = [(t, o) for t in range(n_col) for o in range(n_half) if t or o]
    for t in range(1, n_col):
        chunk(t)
        psend[t - 1] = acc[...].astype(jnp.bfloat16)
        part_copy(t).start()
        for o in range(n_half):
            norm_copy(t, o).start()
    chunk(0)
    for o in range(1, n_half):
        norm_copy(0, o).start()
    total = acc[...]
    for t in range(1, n_col):
        part_copy(t).wait()
        total += precv[t - 1].astype(jnp.float32)
    asend[...] = total.reshape(groups, depth, share).astype(jnp.bfloat16)
    far_first = sorted(range(1, groups), key=lambda o: -min(o // n_half, n_row - o // n_half))
    for o in far_first:
        piece_copy(o).start()
    norms = nsend[0]
    for t, o in norm_copies:
        norm_copy(t, o).wait()
        norms += nrecv[t, o]
    scale = lax.rsqrt(norms + 1e-06)
    for o in [0] + far_first[::-1]:
        if o:
            piece_copy(o).wait()
        g = lax.rem(me + groups - o, groups)
        piece = arecv[o] if o else asend[me]
        out[0, g // n_half, lax.rem(g, n_half)] = (piece.astype(jnp.float32) * scale).astype(jnp.bfloat16)


def body(vecs, poles, weights, kept, roots, order):
    n_row, n_col, n_half = (lax.axis_size(a) for a in ("row", "col", "half"))
    nrows, cols = vecs.shape[1:]
    panel = order.shape[0]
    share, groups = panel // n_col, n_row * n_half
    depth = nrows // groups
    block = min(4096, cols // 2)
    rows = min(128, share)
    vmem = pl.BlockSpec(memory_space=pltpu.VMEM)
    dma = pltpu.SemaphoreType.DMA
    others = max(n_col - 1, 1)
    return pl.pallas_call(
        functools.partial(kernel, (n_row, n_col, n_half, cols, panel, block, rows)),
        out_shape=jax.ShapeDtypeStruct((1, n_row, n_half, depth, share), jnp.bfloat16),
        in_specs=[pl.BlockSpec(memory_space=pl.ANY)] * 6,
        out_specs=vmem,
        scratch_shapes=[
            pltpu.VMEM((cols // LANES, nrows, LANES), jnp.bfloat16),
            pltpu.VMEM((n_row, 1, panel // n_row), jnp.float32),
            pltpu.VMEM((panel, LANES), jnp.float32),
            pltpu.VMEM((1, cols), jnp.float32),
            pltpu.VMEM((1, panel), jnp.int32),
            pltpu.VMEM((1, cols), jnp.float32),
            pltpu.VMEM((1, cols), jnp.int32),
            pltpu.VMEM((1, cols), jnp.float32),
            pltpu.VMEM((1, panel // n_row), jnp.float32),
            pltpu.VMEM((block // LANES, share, LANES), jnp.bfloat16),
            pltpu.VMEM((block // LANES, share, LANES), jnp.bfloat16),
            pltpu.VMEM((nrows, share), jnp.float32),
            pltpu.VMEM((share, LANES), jnp.float32),
            pltpu.VMEM((others, nrows, share), jnp.bfloat16),
            pltpu.VMEM((others, nrows, share), jnp.bfloat16),
            pltpu.VMEM((n_col, 1, share), jnp.float32),
            pltpu.VMEM((n_col, n_half, 1, share), jnp.float32),
            pltpu.VMEM((groups, depth, share), jnp.bfloat16),
            pltpu.VMEM((groups, depth, share), jnp.bfloat16),
            dma((5,)),
            dma((cols // block,)),
            dma((n_row,)),
            dma((n_row,)),
            dma((others,)),
            dma((others,)),
            dma((n_col, n_half)),
            dma((n_col, n_half)),
            dma((groups,)),
            dma((groups,)),
        ],
        compiler_params=pltpu.CompilerParams(collective_id=0, has_side_effects=True),
        name="merge",
    )(vecs, poles, weights, kept, roots[None, :], order[None, :])


def solution(mesh):
    return jax.shard_map(
        body,
        mesh=mesh,
        in_specs=(
            P(("grp", "half"), "row", "col"),
            P(("grp", "half"), "col"),
            P(("grp", "half"), "col"),
            P(("grp", "half"), "col"),
            P(("grp", "row")),
            P("grp"),
        ),
        out_specs=P(("grp", "row", "half"), None, None, None, "col"),
        check_vma=False,
    )
```
